128 devices in a mesh: ord: 64 (over x, y, z), rhs: 2 (over core).
Axes of the slice: x: 4, y: 4, z: 4, core: 2. Of those that a mesh axis runs over, the one named last changes fastest.
Arguments:
- rhs_blocks: float32 [512, 640, 128], P('ord', None, 'rhs'), may hold values from -6 to 6
- rhs_border: float32 [512, 128], P(None, 'rhs'), may hold values from -6 to 6
- start_blocks: float32 [512, 640, 128], P('ord', None, 'rhs'), may hold values from -3 to 3
- start_border: float32 [512, 128], P(None, 'rhs'), may hold values from -3 to 3
- diag_blocks: bfloat16 [512, 640, 640], P('ord'), may hold values from -1 to 9
- block_inverses: bfloat16 [512, 640, 640], P('ord'), may hold values from -6 to 6
- couplings: bfloat16 [512, 640, 640], P('ord'), may hold values from -0.125 to 0.125
- border_couplings: bfloat16 [512, 640, 512], P('ord'), may hold values from -0.009765625 to 0.009765625
- border_block: bfloat16 [512, 512], replicated, may hold values from -1 to 9
- schur_inverse: float32 [512, 512], replicated, may hold values from -6 to 6
- row_counts: int32 [512], P('ord'), may hold values from 1 to 640, as said below
Outputs:
- solution_blocks: float32 [512, 640, 128], P('ord', None, 'rhs')
- solution_border: float32 [512, 128], P(None, 'rhs')
The draws below stay inside these ranges and needn't reach their ends.
Inputs may be any that keep to these rules, and one draw needn't show every extreme that they name: row_counts[m] is the number of live rows of order block m; block 0 has exactly 640 rows and the counts fall with the order to about a third of 640.
All inputs are finite; a program needn't handle non-finite values.
Results may differ from the reference program's by a relative error of at most 0.0035.
Values may be sent and summed in bfloat16 or wider, within the bound.
No kernel may reach another device: no remote copies, remote signals or barrier semaphores. Data moves between devices by JAX's collectives and lax.ppermute only.
A program may use at most 128 MiB of HBM per device.

```python
import math
import jax
import jax.numpy as jnp
from jax import lax

BR = 640
NB = 512
RHS = 128
ITERS = 3
MB = 512


def dominant_pair(base_key, mat_order, lead_shape):
    scale_key = jax.random.fold_in(base_key, 11)
    noise_key = jax.random.fold_in(base_key, 12)
    low_end, high_end = (1.0, 4.0)
    vec_shape = tuple(lead_shape) + (mat_order,)
    diagonal = jnp.exp(jax.random.uniform(scale_key, vec_shape, jnp.float32, math.log(low_end), math.log(high_end)))
    coupled = jnp.clip(jax.random.normal(noise_key, tuple(lead_shape) + (mat_order, mat_order), jnp.float32), -4.0, 4.0)
    coupled = (coupled + jnp.swapaxes(coupled, -1, -2)) * (0.5 / math.sqrt(2.0 * mat_order))
    identity = jnp.eye(mat_order, dtype=jnp.float32)
    matrix = coupled + diagonal[..., :, None] * identity
    reciprocal = 1.0 / diagonal
    inverse = reciprocal[..., :, None] * identity - reciprocal[..., :, None] * coupled * reciprocal[..., None, :]
    return (matrix, inverse)


def draw_diag_blocks(key, part):
    matrix, inverse = dominant_pair(jax.random.fold_in(key, 101), BR, (MB,))
    return matrix.astype(jnp.bfloat16)


def draw_block_inverses(key, part):
    matrix, inverse = dominant_pair(jax.random.fold_in(key, 101), BR, (MB,))
    return inverse.astype(jnp.bfloat16)


def draw_border_block(key, part):
    matrix, inverse = dominant_pair(jax.random.fold_in(key, 202), NB, ())
    return matrix.astype(jnp.bfloat16)


def draw_schur_inverse(key, part):
    matrix, inverse = dominant_pair(jax.random.fold_in(key, 202), NB, ())
    return inverse.astype(jnp.float32)


def draw_row_counts(key, part):
    blocks = jnp.arange(MB, dtype=jnp.int32)
    falling = blocks * (2 * BR // 3) // MB
    jitter = jax.random.randint(jax.random.fold_in(key, 303), (MB,), 0, BR // 16 + 1, dtype=jnp.int32)
    jitter = jnp.where(blocks == 0, 0, jitter)
    return (BR - falling - jitter).astype(jnp.int32)


def block_levels(key, shape, split, low, largest):
    level = 1.0
    for axis_at, parts in split:
        heights = jax.random.uniform(jax.random.fold_in(jax.random.fold_in(key, 6), axis_at), (parts,), jnp.float32, low / len(split), largest / len(split))
        level = level * jnp.repeat(jnp.exp(heights), shape[axis_at] // parts).reshape((-1,) + (1,) * (len(shape) - 1 - axis_at))
    return level


def scatter_about(rng, extent, spread, reach, shards=(), kind=jnp.bfloat16):
    drawn = spread * jax.random.normal(rng, extent, jnp.float32)
    if shards:
        drawn = drawn * block_levels(rng, extent, shards, -0.22, 0.18)
    return jnp.clip(drawn, -reach, reach).astype(kind)


def setup_inputs(seed: int = 0) -> dict:
    streams_of = jax.random.split(jax.random.key(seed), 12)
    rhs_blocks = scatter_about(streams_of[0], (MB, BR, RHS), 1.0, 6.0, ((0, 64), (2, 2)), jnp.float32)
    rhs_border = scatter_about(streams_of[1], (NB, RHS), 1.0, 6.0, ((1, 2),), jnp.float32)
    start_blocks = scatter_about(streams_of[2], (MB, BR, RHS), 0.5, 3.0, ((0, 64), (2, 2)), jnp.float32)
    start_border = scatter_about(streams_of[3], (NB, RHS), 0.5, 3.0, ((1, 2),), jnp.float32)
    diag_blocks = draw_diag_blocks(jax.random.fold_in(streams_of[11], 71), 0)
    block_inverses = draw_block_inverses(jax.random.fold_in(streams_of[11], 71), 0)
    couplings = scatter_about(streams_of[6], (MB, BR, BR), (4 * BR) ** -0.5, 0.125, ((0, 64),))
    border_couplings = scatter_about(streams_of[7], (MB, BR, NB), (BR * MB) ** -0.5, 0.009765625, ((0, 64),))
    border_block = draw_border_block(jax.random.fold_in(streams_of[11], 71), 0)
    schur_inverse = draw_schur_inverse(jax.random.fold_in(streams_of[11], 71), 0)
    row_counts = draw_row_counts(jax.random.fold_in(streams_of[11], 71), 0)
    return dict(rhs_blocks=rhs_blocks, rhs_border=rhs_border, start_blocks=start_blocks, start_border=start_border, diag_blocks=diag_blocks, block_inverses=block_inverses, couplings=couplings, border_couplings=border_couplings, border_block=border_block, schur_inverse=schur_inverse, row_counts=row_counts)


def widen(array):
    return array.astype(jnp.float32)


def rounded(array):
    return lax.optimization_barrier(array.astype(jnp.bfloat16)).astype(jnp.float32)


def batched(matrices, vectors):
    return jnp.einsum('mij,mjc->mic', matrices, vectors, precision=lax.Precision.HIGHEST)


def reference(rhs_blocks, rhs_border, start_blocks, start_border, diag_blocks, block_inverses, couplings, border_couplings, border_block, schur_inverse, row_counts):
    live_rows = (jnp.arange(BR, dtype=jnp.int32)[None, :] < row_counts[:, None]).astype(jnp.float32)[:, :, None]
    wide_diag = widen(diag_blocks)
    wide_inverse = widen(block_inverses)
    wide_coupling = widen(couplings)
    wide_border = widen(border_couplings)

    def operate(state, state_border):
        wide_state = rounded(state)
        narrow_border = state_border.astype(jnp.bfloat16)
        following = jnp.concatenate([wide_state[1:], jnp.zeros_like(wide_state[:1])], 0)
        ahead = batched(wide_coupling, following)
        transposed = jnp.einsum('mji,mjc->mic', wide_coupling, wide_state, precision=lax.Precision.HIGHEST)
        behind = jnp.concatenate([jnp.zeros_like(transposed[:1]), transposed[:-1]], 0)
        from_border = jnp.einsum('mib,bc->mic', wide_border, widen(narrow_border), precision=lax.Precision.HIGHEST)
        applied = live_rows * (batched(wide_diag, wide_state) + ahead + behind + from_border)
        gathered = jnp.einsum('mib,mic->bc', wide_border, wide_state, precision=lax.Precision.HIGHEST)
        applied_border = jnp.dot(border_block, narrow_border, preferred_element_type=jnp.float32) + gathered
        return applied, applied_border

    def precondition(residual, resid_border):
        blockwise = live_rows * batched(wide_inverse, rounded(residual))
        border_sum = jnp.einsum('mib,mic->bc', wide_border, rounded(blockwise), precision=lax.Precision.HIGHEST)
        update_border = jnp.dot(schur_inverse, resid_border - border_sum, precision=lax.Precision.HIGHEST)
        lifted = rounded(jnp.einsum('mib,bc->mic', wide_border, rounded(update_border), precision=lax.Precision.HIGHEST))
        update = blockwise - live_rows * batched(wide_inverse, lifted)
        return update, update_border

    solution = live_rows * start_blocks
    solution_border = start_border
    applied, applied_border = operate(solution, solution_border)
    residual = live_rows * rhs_blocks - applied
    resid_border = rhs_border - applied_border
    for iteration in range(ITERS):
        update, update_border = precondition(residual, resid_border)
        applied, applied_border = operate(update, update_border)
        numerator = jnp.sum(residual * applied) + jnp.sum(resid_border * applied_border)
        denominator = jnp.sum(applied * applied) + jnp.sum(applied_border * applied_border)
        step_size = numerator / (denominator + 1e-6)
        solution = solution + step_size * update
        solution_border = solution_border + step_size * update_border
        residual = residual - step_size * applied
        resid_border = resid_border - step_size * applied_border
    return solution, solution_border
```

```python
import functools

import jax
import jax.numpy as jnp
from jax import lax
from jax.experimental import pallas as pl
from jax.experimental.pallas import tpu as pltpu
from jax.sharding import Mesh
from jax.sharding import PartitionSpec as P

ITERS = 3
AXES = ("ord_0", "ord_1", "ord_2")
F32, BF16 = jnp.float32, jnp.bfloat16
SIDE = 4
WIRE = (F32, F32, BF16, BF16)
MIB = 1 << 20


def nt(a, b):
    return lax.dot_general(a, b, (((1,), (1,)), ((), ())), preferred_element_type=F32)


def nn(a, b):
    return lax.dot_general(a, b, (((1,), (0,)), ((), ())), preferred_element_type=F32)


def nt_full(a, b):
    return lax.dot_general(
        a, b, (((1,), (1,)), ((), ())), precision=lax.Precision.HIGHEST, preferred_element_type=F32
    )


def two_parts(value):
    high = value.astype(BF16)
    low = (value - high.astype(F32)).astype(BF16)
    return jnp.concatenate([high, low], 0)


def nt_wide(value, b):
    rows = value.shape[0]
    both = nt(two_parts(value), b)
    return both[:rows] + both[rows:]


def live_row(counts, m, rows):
    return (lax.broadcasted_iota(jnp.int32, (1, rows), 1) < counts[m]).astype(F32)


def total(value):
    return jnp.sum(value, keepdims=True)


def call(kernel, outs, args, spaces, scratch=(), limit=16, flops=10**8):
    where = {"v": pltpu.VMEM, "m": pltpu.VMEM, "s": pltpu.SMEM}
    args = [
        pltpu.with_memory_space_constraint(a, pltpu.VMEM) if s == "m" else a
        for a, s in zip(args, spaces, strict=True)
    ]
    return pl.pallas_call(
        kernel,
        out_shape=[jax.ShapeDtypeStruct(*o) for o in outs],
        in_specs=[pl.BlockSpec(memory_space=where[s]) for s in spaces],
        out_specs=[pl.BlockSpec(memory_space=pltpu.VMEM)] * len(outs),
        scratch_shapes=list(scratch),
        compiler_params=pltpu.CompilerParams(vmem_limit_bytes=limit * MIB),
        cost_estimate=pl.CostEstimate(flops=flops, bytes_accessed=10**6, transcendentals=0),
    )(*args)


def tail_rows(dtype):
    return 8 if dtype == F32 else 16


def scalar_tile(num, den, dtype):
    row = lax.broadcasted_iota(jnp.int32, (tail_rows(dtype), 128), 0)
    if dtype == F32:
        return jnp.where(row == 0, num, jnp.where(row == 1, den, 0.0))
    num_high, den_high = num.astype(BF16).astype(F32), den.astype(BF16).astype(F32)
    parts = (num_high, num - num_high, den_high, den - den_high)
    tile = jnp.zeros((tail_rows(dtype), 128), F32)
    for i, part in enumerate(parts):
        tile = jnp.where(row == i, part, tile)
    return tile.astype(BF16)


def scalars_of(tile):
    if tile.shape[0] == 8:
        return tile[0:1], tile[1:2]
    return tile[0:1] + tile[1:2], tile[2:3] + tile[3:4]


def emit(me, sums, outs, num, den):
    share = sums[0].shape[0] // SIDE
    for k, out in enumerate(outs):
        first = pl.multiple_of(lax.rem(me + k, SIDE) * share, share)
        row = 0
        for chunk in range(sums[0].shape[1] // 128):
            for one in sums:
                out[row : row + share, :] = one[pl.ds(first, share), chunk * 128 : chunk * 128 + 128].astype(out.dtype)
                row += share
        out[row:, :] = scalar_tile(num, den, out.dtype)


def added(parts):
    p = [part[...].astype(F32) for part in parts]
    return (p[0] + p[2]) + (p[1] + p[3])


def sum_kernel(a, b, c, d, out):
    value = added((a, b, c, d))
    tail = tail_rows(out.dtype)
    out[:-tail, :] = value[:-tail].astype(out.dtype)
    num, den = scalars_of(value[-tail:])
    out[-tail:, :] = scalar_tile(num, den, out.dtype)


def combined(parts):
    first = parts[0]
    return call(sum_kernel, [(first.shape, first.dtype)], parts, "vvvv", limit=4, flops=10**5)[0]


def swapped(values, axis):
    got = [values[0]]
    for k in range(1, SIDE):
        got.append(lax.ppermute(values[k], axis, [(i, (i + k) % SIDE) for i in range(SIDE)]))
    return got


def reduced(shares):
    mine = combined(swapped(shares, AXES[0]))
    mine = combined(swapped([mine] * SIDE, AXES[1]))
    return swapped([mine] * SIDE, AXES[2])


def unpacked(value, count, chunks=4):
    tail = value.shape[0] % 32 or 16
    share = (value.shape[0] - tail) // (count * chunks)
    arrays = []
    for i in range(count):
        pieces = [value[(c * count + i) * share : (c * count + i + 1) * share] for c in range(chunks)]
        arrays.append(jnp.concatenate(pieces, 1))
    return arrays, scalars_of(value[-tail:])


def edge_start(counts, x, e, up, down):
    last = x.shape[0] - 1
    rows = x.shape[2]
    up[...] = (x[0] * live_row(counts, 0, rows)).astype(BF16)
    tail = (x[last] * live_row(counts, last, rows)).astype(BF16)
    down[...] = nn(tail, e[last]).astype(BF16)


def inner_start(counts, x, b, border, d, e, c, inv, r, y, edge, t, g, v):
    slots, _, rows = x.shape
    for m in range(slots):
        v[m] = (x[m] * live_row(counts, m, rows)).astype(BF16)
    narrow = border[...].astype(BF16)
    t[...] = jnp.zeros_like(t)
    g[...] = jnp.zeros_like(g)

    @pl.loop(1, slots - 1)
    def _(m):
        live = live_row(counts, m, rows)
        q = nt(v[m], d[m]) + nt(v[m + 1], e[m]) + nn(v[m - 1], e[m - 1]) + nt(narrow, c[m])
        res = live * (b[m] - q)
        blockwise = live * nt_wide(res, inv[m])
        r[m - 1] = res
        y[m - 1] = blockwise
        both = nn(jnp.concatenate([blockwise.astype(BF16), v[m]], 0), c[m])
        t[...] += both[: t.shape[0]]
        g[...] += both[t.shape[0] :]

    z = slots - 1
    edge[0] = nt(v[0], d[0]) + nt(v[1], e[0]) + nt(narrow, c[0])
    edge[1] = nt(v[z], d[z]) + nn(v[z - 1], e[z - 1]) + nt(narrow, c[z])


def outer_start(counts, me, x, b, edge, up, down, e, c, inv, t_in, g_in, r, y, s0, s1, s2, s3, t, g):
    slots, _, rows = x.shape
    z = slots - 1
    t[...] = t_in[...]
    g[...] = g_in[...]
    for i, m in enumerate((0, z)):
        live = live_row(counts, m, rows)
        other = down[...].astype(F32) if i == 0 else nt(up[...], e[z])
        res = live * (b[m] - (edge[i] + other))
        blockwise = live * nt_wide(res, inv[m])
        r[i] = res
        y[i] = blockwise
        v = (x[m] * live).astype(BF16)
        both = nn(jnp.concatenate([blockwise.astype(BF16), v], 0), c[m])
        t[...] += both[: t.shape[0]]
        g[...] += both[t.shape[0] :]
    zero = jnp.zeros((1, 1), F32)
    emit(me[0], (t, g), (s0, s1, s2, s3), zero, zero)


def border_start(me, p0, p1, p2, p3, rhs, border, bb, out, target):
    (s, g), _ = unpacked(added((p0, p1, p2, p3)), 2)
    share = s.shape[0]
    mine = pl.ds(pl.multiple_of(me[0] * share, share), share)
    left = rhs[mine, :] - nt(border[mine, :].astype(BF16), bb[...]) - g
    out[...] = left
    target[...] = left - s


def border_step(me, p0, p1, p2, p3, rb, wb, bb, out, diff, scal):
    arrays, (num, den) = unpacked(added((p0, p1, p2, p3)), 2 if diff is not None else 1)
    g = arrays[-1]
    share = g.shape[0]
    mine = pl.ds(pl.multiple_of(me[0] * share, share), share)
    q = nt(wb[mine, :].astype(BF16), bb[...]) + g
    out[...] = q
    if diff is not None:
        diff[...] = q - arrays[0]
    row = lax.broadcasted_iota(jnp.int32, scal.shape, 0)
    num = num * (1.0 / SIDE) + total(rb[...] * q)
    den = den * (1.0 / SIDE) + total(q * q)
    scal[...] = jnp.where(row == 0, num, jnp.where(row == 1, den, 0.0))


def border_last(me, p0, p1, p2, p3, rb, wb, bb, out, scal):
    border_step(me, p0, p1, p2, p3, rb, wb, bb, out, None, scal)


def solve(target, s, out):
    out[...] = nt_full(target[...], s[...])


def step_of(parts, border):
    tile = added([part.at[:, border : border + 128] for part in parts])
    return tile[0:1] / (tile[1:2] + 1e-06)


def place(me, parts, wb, scale, old):
    share = parts[0].shape[0]
    border = wb.shape[1]
    for k, part in enumerate(parts):
        rows = pl.ds(pl.multiple_of(lax.rem(me + SIDE - k, SIDE) * share, share), share)
        if old is None:
            wb[rows, :] = part[:, :border]
        else:
            wb[rows, :] = old[rows, :] + scale * part[:, :border]


def edge_update(counts, narrow, yv, c, inv, e, w, u, up, down, slots, rows):
    z = slots - 1
    for i, m in enumerate((0, z)):
        live = live_row(counts, m, rows)
        lift = nt(narrow, c[m])
        u[i] = lift
        value = yv[i] - live * nt(lift.astype(BF16), inv[m])
        w[i] = value
        if i == 0:
            up[...] = value.astype(BF16)
        else:
            down[...] = nn(value.astype(BF16), e[z]).astype(BF16)


def edge_first(counts, me, a0, a1, a2, a3, y, c, inv, e, wb, w, u, up, down):
    place(me[0], (a0, a1, a2, a3), wb, None, None)
    yv = [y[0], y[1]]
    edge_update(counts, wb[...].astype(BF16), yv, c, inv, e, w, u, up, down, inv.shape[0], inv.shape[1])


def edge_next(
    counts, me, a0, a1, a2, a3, wb_in, sol_in, rb_in, qb, y_in, p, r_in, q, c, inv, e,
    alpha, wb, sol, rb, y, r, w, u, up, down,
):
    parts = (a0, a1, a2, a3)
    border = wb.shape[1]
    step = step_of(parts, border)
    alpha[...] = jnp.broadcast_to(step, alpha.shape)
    a = step[:, :1]
    sol[...] = sol_in[...] + a * wb_in[...]
    place(me[0], parts, wb, -a, wb_in)
    rb[...] = rb_in[...] - a * qb[...]
    yv = []
    for i in range(2):
        r[i] = r_in[i] - a * q[i]
        value = y_in[i] - a * p[i]
        y[i] = value
        yv.append(value)
    edge_update(counts, wb[...].astype(BF16), yv, c, inv, e, w, u, up, down, inv.shape[0], inv.shape[1])


def inner_body(counts, load, narrow, w_edge, u_edge, d, e, c, inv, w, q, p, edge, t, g, num, den, v, u, keep):
    slots, rows, _ = inv.shape
    z = slots - 1
    v[0] = w_edge[0].astype(BF16)
    v[z] = w_edge[1].astype(BF16)

    @pl.loop(1, z)
    def _(m):
        live = live_row(counts, m, rows)
        lift = nt(narrow, c[m])
        u[m] = lift
        value = load(m) - live * nt(lift.astype(BF16), inv[m])
        w[m - 1] = value
        v[m] = value.astype(BF16)

    if t is not None:
        t[...] = jnp.zeros_like(t)
    g[...] = jnp.zeros_like(g)
    num[...] = jnp.zeros_like(num)
    den[...] = jnp.zeros_like(den)

    @pl.loop(1, z)
    def _(m):
        live = live_row(counts, m, rows)
        value = live * (nt(v[m], d[m]) + nt(v[m + 1], e[m]) + nn(v[m - 1], e[m - 1]) + u[m])
        num[...] += jnp.sum(keep(m) * value, 0, keepdims=True)
        den[...] += jnp.sum(value * value, 0, keepdims=True)
        if t is None:
            g[...] += nn(v[m], c[m])
        else:
            q[m - 1] = value
            back = live * nt_wide(value, inv[m])
            p[m - 1] = back
            both = nn(jnp.concatenate([back.astype(BF16), v[m]], 0), c[m])
            t[...] += both[: t.shape[0]]
            g[...] += both[t.shape[0] :]

    edge[0] = nt(v[0], d[0]) + nt(v[1], e[0]) + u_edge[0]
    edge[1] = nt(v[z], d[z]) + nn(v[z - 1], e[z - 1]) + u_edge[1]


def inner_first(counts, wb, w_edge, u_edge, y, r, d, e, c, inv, w, q, p, edge, t, g, num, den, v, u):
    inner_body(
        counts, lambda m: y[m - 1], wb[...].astype(BF16), w_edge, u_edge, d, e, c, inv,
        w, q, p, edge, t, g, num, den, v, u, lambda m: r[m - 1],
    )


def inner_next(
    counts, alpha, wb, w_edge, u_edge, y_in, p_in, r_in, q_in, d, e, c, inv,
    y, r, w, q, p, edge, t, g, num, den, v, u,
):
    a = alpha[0:1, 0:1]

    def load(m):
        y[m - 1] = y_in[m - 1] - a * p_in[m - 1]
        r[m - 1] = r_in[m - 1] - a * q_in[m - 1]
        return y[m - 1]

    inner_body(
        counts, load, wb[...].astype(BF16), w_edge, u_edge, d, e, c, inv,
        w, q, p, edge, t, g, num, den, v, u, lambda m: r[m - 1],
    )


def inner_last(
    counts, alpha, wb, w_edge, u_edge, y_in, p_in, r_in, q_in, d, e, c, inv,
    w, edge, g, num, den, v, u,
):
    a = alpha[0:1, 0:1]
    inner_body(
        counts, lambda m: y_in[m - 1] - a * p_in[m - 1], wb[...].astype(BF16), w_edge, u_edge, d, e, c, inv,
        w, None, None, edge, None, g, num, den, v, u, lambda m: r_in[m - 1] - a * q_in[m - 1],
    )


def outer_body(counts, me, w_edge, r_edge, edge, up, down, e, c, inv, t_in, g_in, num_in, den_in, q, p, shares, t, g):
    slots, rows, _ = inv.shape
    z = slots - 1
    if t is not None:
        t[...] = t_in[...]
    g[...] = g_in[...]
    num, den = total(num_in[...]), total(den_in[...])
    for i, m in enumerate((0, z)):
        live = live_row(counts, m, rows)
        other = down[...].astype(F32) if i == 0 else nt(up[...], e[z])
        value = live * (edge[i] + other)
        num += total(r_edge[i] * value)
        den += total(value * value)
        v = w_edge[i].astype(BF16)
        if t is None:
            g[...] += nn(v, c[m])
        else:
            q[i] = value
            back = live * nt_wide(value, inv[m])
            p[i] = back
            both = nn(jnp.concatenate([back.astype(BF16), v], 0), c[m])
            t[...] += both[: t.shape[0]]
            g[...] += both[t.shape[0] :]
    emit(me[0], (g,) if t is None else (t, g), shares, num, den)


def outer_step(counts, me, w_edge, r_edge, edge, up, down, e, c, inv, t_in, g_in, num, den, q, p, s0, s1, s2, s3, t, g):
    outer_body(
        counts, me, w_edge, r_edge, edge, up, down, e, c, inv, t_in, g_in, num, den, q, p, (s0, s1, s2, s3), t, g
    )


def outer_last(counts, me, w_edge, r_edge, edge, up, down, e, c, inv, g_in, num, den, s0, s1, s2, s3, g):
    outer_body(
        counts, me, w_edge, r_edge, edge, up, down, e, c, inv, None, g_in, num, den, None, None,
        (s0, s1, s2, s3), None, g,
    )


def finish(counts, a0, a1, a2, a3, wb, sol, x, al0, al1, e0, e1, e2, w0, w1, w2, out, border):
    slots, _, rows = x.shape
    step = step_of((a0, a1, a2, a3), 0)[:, :1]
    border[...] = sol[...] + step * wb[...]
    c0, c1 = al0[0:1, 0:1], al1[0:1, 0:1]
    for m in range(slots):
        if m in (0, slots - 1):
            i = 0 if m == 0 else 1
            a, b, c = e0[i], e1[i], e2[i]
        else:
            a, b, c = w0[m - 1], w1[m - 1], w2[m - 1]
        out[m] = ((x[m] * live_row(counts, m, rows) + c0 * a) + c1 * b) + step * c


def halo(up, down):
    count = lax.axis_size(AXES)
    ahead = lax.ppermute(up, AXES, [(i + 1, i) for i in range(count - 1)])
    behind = lax.ppermute(down, AXES, [(i, i + 1) for i in range(count - 1)])
    return ahead, behind


def shards(
    rhs_blocks, rhs_border, start_blocks, start_border,
    diag, inverse, coupling, border_coupling, border_block, schur, counts,
):
    x = start_blocks.transpose(0, 2, 1)
    b = rhs_blocks.transpose(0, 2, 1)
    border_rhs, border_x = rhs_border.T, start_border.T
    slots, columns, rows = x.shape
    border = border_x.shape[1]
    share = columns // SIDE
    me = lax.axis_index(AXES[0]).reshape(1).astype(jnp.int32)
    state, edges = ((slots - 2, columns, rows), F32), ((2, columns, rows), F32)
    one16, wide = ((columns, rows), BF16), ((columns, border), F32)
    line, piece = ((1, rows), F32), ((share, border), F32)
    tile = ((8, 128), F32)
    keep16 = pltpu.VMEM((slots, columns, rows), BF16)
    keep32 = pltpu.VMEM((slots, columns, rows), F32)
    acc = pltpu.VMEM((columns, border), F32)

    def message(dtype, sums):
        return ((share * sums * border // 128 + tail_rows(dtype), 128), dtype)

    up, down = call(edge_start, [one16, one16], [counts, x, coupling], "svm")
    up, down = halo(up, down)
    r, y, edge, t, g = call(
        inner_start,
        [state, state, edges, wide, wide],
        [counts, x, b, border_x, diag, coupling, border_coupling, inverse],
        "svvvmmmm",
        [keep16],
        flops=4 * 10**9,
    )
    r_edge, y_edge, *shares = call(
        outer_start,
        [edges, edges] + [message(WIRE[0], 2)] * SIDE,
        [counts, me, x, b, edge, up, down, coupling, border_coupling, inverse, t, g],
        "ssvvvvvmmmvv",
        [acc, acc],
        flops=5 * 10**8,
    )
    parts = reduced(shares)
    rb, target = call(
        border_start, [piece, piece], [me, *parts, border_rhs, border_x, border_block], "sv" + "v" * 6
    )
    found = call(solve, [piece], [target, schur], "vv")[0]
    gathered = swapped([found] * SIDE, AXES[0])

    steps, edge_updates, updates = [], [], []
    sol = border_x
    for k in range(ITERS):
        last = k == ITERS - 1
        if k == 0:
            wb, w_edge, u_edge, up, down = call(
                edge_first,
                [wide, edges, edges, one16, one16],
                [counts, me, *gathered, y_edge, border_coupling, inverse, coupling],
                "ssvvvvvmmm",
                flops=5 * 10**8,
            )
        else:
            step, wb, sol, rb, y_edge, r_edge, w_edge, u_edge, up, down = call(
                edge_next,
                [tile, wide, wide, piece, edges, edges, edges, edges, one16, one16],
                [counts, me, *gathered, wb, sol, rb, qb, y_edge, p_edge, r_edge, q_edge]
                + [border_coupling, inverse, coupling],
                "ss" + "v" * 12 + "mmm",
                flops=5 * 10**8,
            )
            steps.append(step)
        up, down = halo(up, down)
        matrices = [diag, coupling, border_coupling, inverse]
        if k == 0:
            w, q, p, edge, t, g, num, den = call(
                inner_first,
                [state, state, state, edges, wide, wide, line, line],
                [counts, wb, w_edge, u_edge, y, r] + matrices,
                "svvvvvmmmm",
                [keep16, keep32],
                flops=4 * 10**9,
            )
        elif not last:
            y, r, w, q, p, edge, t, g, num, den = call(
                inner_next,
                [state, state, state, state, state, edges, wide, wide, line, line],
                [counts, step, wb, w_edge, u_edge, y, p, r, q] + matrices,
                "s" + "v" * 8 + "mmmm",
                [keep16, keep32],
                limit=24,
                flops=4 * 10**9,
            )
        else:
            w, edge, g, num, den = call(
                inner_last,
                [state, edges, wide, line, line],
                [counts, step, wb, w_edge, u_edge, y, p, r, q] + matrices,
                "s" + "v" * 8 + "mmmm",
                [keep16, keep32],
                flops=3 * 10**9,
            )
        edge_updates.append(w_edge)
        updates.append(w)
        inputs = [counts, me, w_edge, r_edge, edge, up, down, coupling, border_coupling, inverse]
        if not last:
            q_edge, p_edge, *shares = call(
                outer_step,
                [edges, edges] + [message(WIRE[k + 1], 2)] * SIDE,
                inputs + [t, g, num, den],
                "ssvvvvvmmmvvvv",
                [acc, acc],
                flops=5 * 10**8,
            )
            parts = reduced(shares)
            qb, diff, scal = call(
                border_step,
                [piece, piece, ((share, 128), F32)],
                [me, *parts, rb, wb, border_block],
                "s" + "v" * 7,
            )
            partner = lax.ppermute(scal, "rhs", [(0, 1), (1, 0)])
            found = call(solve, [piece], [diff, schur], "vv")[0]
            sent = jnp.concatenate([found, scal + partner], 1)
        else:
            shares = call(
                outer_last,
                [message(WIRE[k + 1], 1)] * SIDE,
                inputs + [g, num, den],
                "ssvvvvvmmmvvv",
                [acc],
                flops=3 * 10**8,
            )
            parts = reduced(shares)
            qb, scal = call(
                border_last,
                [piece, ((share, 128), F32)],
                [me, *parts, rb, wb, border_block],
                "s" + "v" * 7,
            )
            partner = lax.ppermute(scal, "rhs", [(0, 1), (1, 0)])
            sent = scal + partner
        gathered = swapped([sent] * SIDE, AXES[0])
    out, border_out = call(
        finish,
        [(x.shape, F32), wide],
        [counts, *gathered, wb, sol, x, *steps, *edge_updates, *updates],
        "s" + "v" * 15,
        limit=24,
    )
    return out.transpose(0, 2, 1), border_out.T


def solution(mesh):
    finer = Mesh(mesh.devices.reshape(SIDE, SIDE, SIDE, mesh.shape["rhs"]), (*AXES, "rhs"))
    return jax.shard_map(
        shards,
        mesh=finer,
        in_specs=(
            P(AXES, None, "rhs"),
            P(None, "rhs"),
            P(AXES, None, "rhs"),
            P(None, "rhs"),
            P(AXES, None, None),
            P(AXES, None, None),
            P(AXES, None, None),
            P(AXES, None, None),
            P(),
            P(),
            P(AXES),
        ),
        out_specs=(P(AXES, None, "rhs"), P(None, "rhs")),
        check_vma=False,
    )
```

```python
import functools

import jax
import jax.numpy as jnp
from jax import lax
from jax.experimental import pallas as pl
from jax.experimental.pallas import tpu as pltpu
from jax.sharding import Mesh
from jax.sharding import PartitionSpec as P

ITERS = 3
AXES = ("ord_0", "ord_1", "ord_2")
F32, BF16 = jnp.float32, jnp.bfloat16
SIDE = 4
WIRE = (F32, F32, BF16, BF16)
MIB = 1 << 20


def nt(a, b):
    return lax.dot_general(a, b, (((1,), (1,)), ((), ())), preferred_element_type=F32)


def nn(a, b):
    return lax.dot_general(a, b, (((1,), (0,)), ((), ())), preferred_element_type=F32)


def nt_full(a, b):
    return lax.dot_general(
        a, b, (((1,), (1,)), ((), ())), precision=lax.Precision.HIGHEST, preferred_element_type=F32
    )


def two_parts(value):
    high = value.astype(BF16)
    low = (value - high.astype(F32)).astype(BF16)
    return jnp.concatenate([high, low], 0)


def nn_wide(value, b):
    rows = value.shape[0]
    both = nn(two_parts(value), b)
    return both[:rows] + both[rows:]


def live_row(counts, m, rows):
    return (lax.broadcasted_iota(jnp.int32, (1, rows), 1) < counts[m]).astype(F32)


def total(value):
    return jnp.sum(value, keepdims=True)


def call(kernel, outs, args, spaces, scratch=(), limit=6, flops=10**8):
    where = {"v": pltpu.VMEM, "m": pltpu.VMEM, "s": pltpu.SMEM}
    args = [
        pltpu.with_memory_space_constraint(a, pltpu.VMEM) if s == "m" else a
        for a, s in zip(args, spaces, strict=True)
    ]
    return pl.pallas_call(
        kernel,
        out_shape=[jax.ShapeDtypeStruct(*o) for o in outs],
        in_specs=[pl.BlockSpec(memory_space=where[s]) for s in spaces],
        out_specs=[pl.BlockSpec(memory_space=pltpu.VMEM)] * len(outs),
        scratch_shapes=list(scratch),
        compiler_params=pltpu.CompilerParams(vmem_limit_bytes=limit * MIB),
        cost_estimate=pl.CostEstimate(flops=flops, bytes_accessed=10**6, transcendentals=0),
    )(*args)


def tail_rows(dtype):
    return 8 if dtype == F32 else 16


def scalar_tile(num, den, dtype):
    row = lax.broadcasted_iota(jnp.int32, (tail_rows(dtype), 128), 0)
    if dtype == F32:
        return jnp.where(row == 0, num, jnp.where(row == 1, den, 0.0))
    num_high, den_high = num.astype(BF16).astype(F32), den.astype(BF16).astype(F32)
    parts = (num_high, num - num_high, den_high, den - den_high)
    tile = jnp.zeros((tail_rows(dtype), 128), F32)
    for i, part in enumerate(parts):
        tile = jnp.where(row == i, part, tile)
    return tile.astype(BF16)


def scalars_of(tile):
    if tile.shape[0] == 8:
        return tile[0:1], tile[1:2]
    return tile[0:1] + tile[1:2], tile[2:3] + tile[3:4]


def emit(me, sums, outs, num, den):
    share = sums[0].shape[0] // SIDE
    for k, out in enumerate(outs):
        first = pl.multiple_of(jnp.bitwise_xor(me, k) * share, share)
        row = 0
        for chunk in range(sums[0].shape[1] // 128):
            for one in sums:
                out[row : row + share, :] = one[pl.ds(first, share), chunk * 128 : chunk * 128 + 128].astype(out.dtype)
                row += share
        out[row:, :] = scalar_tile(num, den, out.dtype)


def added(parts):
    p = [part[...].astype(F32) for part in parts]
    return (p[0] + p[1]) + (p[2] + p[3])


def sum_kernel(a, b, c, d, out):
    value = added((a, b, c, d))
    tail = tail_rows(out.dtype)
    out[:-tail, :] = value[:-tail].astype(out.dtype)
    num, den = scalars_of(value[-tail:])
    out[-tail:, :] = scalar_tile(num, den, out.dtype)


def combined(parts):
    first = parts[0]
    return call(sum_kernel, [(first.shape, first.dtype)], parts, "vvvv", limit=4, flops=10**5)[0]


def swapped(values, axis):
    got = [values[0]]
    for k in range(1, SIDE):
        got.append(lax.ppermute(values[k], axis, [(i, i ^ k) for i in range(SIDE)]))
    return got


def reduced(shares):
    mine = combined(swapped(shares, AXES[0]))
    mine = combined(swapped([mine] * SIDE, AXES[1]))
    return swapped([mine] * SIDE, AXES[2])


def unpacked(value, count, chunks=4):
    tail = value.shape[0] % 32 or 16
    share = (value.shape[0] - tail) // (count * chunks)
    arrays = []
    for i in range(count):
        pieces = [value[(c * count + i) * share : (c * count + i + 1) * share] for c in range(chunks)]
        arrays.append(jnp.concatenate(pieces, 1))
    return arrays, scalars_of(value[-tail:])


def load(d_in, e_in, c_in, inv_in, dt, et, e, ct, c, invt, stage, sems):
    slots = e.shape[0]

    def copies(m):
        slot = lax.rem(m, 2)
        return (
            pltpu.make_async_copy(d_in.at[m], stage.at[0, slot], sems.at[0, slot]),
            pltpu.make_async_copy(inv_in.at[m], stage.at[1, slot], sems.at[1, slot]),
            pltpu.make_async_copy(e_in.at[m], e.at[m], sems.at[2, slot]),
            pltpu.make_async_copy(c_in.at[m], c.at[m], sems.at[3, slot]),
        )

    for copy in copies(0):
        copy.start()

    @pl.loop(0, slots)
    def _(m):
        @pl.when(m + 1 < slots)
        def _():
            for copy in copies(m + 1):
                copy.start()

        for copy in copies(m):
            copy.wait()
        slot = lax.rem(m, 2)
        dt[m] = stage[0, slot].T
        invt[m] = stage[1, slot].T
        et[m] = e[m].T
        ct[m] = c[m].T


def resident(diag, coupling, border_coupling, inverse):
    slots, rows, border = border_coupling.shape
    square, tall, flat = (slots, rows, rows), (slots, rows, border), (slots, border, rows)
    shapes = (square, square, square, flat, tall, square)
    return pl.pallas_call(
        load,
        out_shape=[pltpu.VMEM(shape, BF16) for shape in shapes],
        in_specs=[pl.BlockSpec(memory_space=pltpu.HBM)] * 4,
        out_specs=[pl.BlockSpec(memory_space=pltpu.VMEM)] * 6,
        scratch_shapes=[pltpu.VMEM((2, 2, rows, rows), BF16), pltpu.SemaphoreType.DMA((4, 2))],
        compiler_params=pltpu.CompilerParams(vmem_limit_bytes=8 * MIB),
        cost_estimate=pl.CostEstimate(flops=10**9, bytes_accessed=25 * 10**6, transcendentals=0),
    )(*(pltpu.with_memory_space_constraint(a, pltpu.HBM) for a in (diag, coupling, border_coupling, inverse)))


def put_halo(odd, up, down, first, second):
    odd = jnp.broadcast_to(odd, up.shape) == 1
    first[...] = jnp.where(odd, up, down).astype(BF16)
    second[...] = jnp.where(odd, down, up).astype(BF16)


def from_halo(odd, first, second):
    a, b = first[...].astype(F32), second[...].astype(F32)
    odd = jnp.broadcast_to(odd, a.shape) == 1
    return jnp.where(odd, b, a).astype(BF16), jnp.where(odd, a, b)


def edge_start(counts, me, x, e, first, second):
    last = x.shape[0] - 1
    rows = x.shape[2]
    tail = (x[last] * live_row(counts, last, rows)).astype(BF16)
    put_halo(me[1], x[0] * live_row(counts, 0, rows), nn(tail, e[0]), first, second)


def inner_start(counts, x, b, border, dt, et, e, ct, c, invt, r, y, edge, t, g, v):
    slots, _, rows = x.shape
    for m in range(slots):
        v[m] = (x[m] * live_row(counts, m, rows)).astype(BF16)
    narrow = border[...].astype(BF16)
    t[...] = jnp.zeros_like(t)
    g[...] = jnp.zeros_like(g)

    @pl.loop(1, slots - 1)
    def _(m):
        live = live_row(counts, m, rows)
        q = nn(v[m], dt[m]) + nn(v[m + 1], et[m]) + nn(v[m - 1], e[m - 1]) + nn(narrow, ct[m])
        res = live * (b[m] - q)
        blockwise = live * nn_wide(res, invt[m])
        r[m - 1] = res
        y[m - 1] = blockwise
        both = nn(jnp.concatenate([blockwise.astype(BF16), v[m]], 0), c[m])
        t[...] += both[: t.shape[0]]
        g[...] += both[t.shape[0] :]

    z = slots - 1
    edge[0] = nn(v[0], dt[0]) + nn(v[1], et[0]) + nn(narrow, ct[0])
    edge[1] = nn(v[z], dt[z]) + nn(v[z - 1], e[z - 1]) + nn(narrow, ct[z])


def outer_start(counts, me, x, b, edge, first, second, et, c, invt, t_in, g_in, r, y, s0, s1, s2, s3, t, g):
    slots, _, rows = x.shape
    z = slots - 1
    t[...] = t_in[...]
    g[...] = g_in[...]
    ahead, behind = from_halo(me[1], first, second)
    for i, m in enumerate((0, z)):
        live = live_row(counts, m, rows)
        other = behind if i == 0 else nn(ahead, et[z])
        res = live * (b[m] - (edge[i] + other))
        blockwise = live * nn_wide(res, invt[m])
        r[i] = res
        y[i] = blockwise
        v = (x[m] * live).astype(BF16)
        both = nn(jnp.concatenate([blockwise.astype(BF16), v], 0), c[m])
        t[...] += both[: t.shape[0]]
        g[...] += both[t.shape[0] :]
    zero = jnp.zeros((1, 1), F32)
    emit(me[0], (t, g), (s0, s1, s2, s3), zero, zero)


def border_start(me, p0, p1, p2, p3, rhs, border, bb, out, target):
    (s, g), _ = unpacked(added((p0, p1, p2, p3)), 2)
    share = s.shape[0]
    mine = pl.ds(pl.multiple_of(me[0] * share, share), share)
    left = rhs[mine, :] - nt(border[mine, :].astype(BF16), bb[...]) - g
    out[...] = left
    target[...] = left - s


def border_step(me, p0, p1, p2, p3, rb, wb, bb, out, diff, scal):
    arrays, (num, den) = unpacked(added((p0, p1, p2, p3)), 2 if diff is not None else 1)
    g = arrays[-1]
    share = g.shape[0]
    mine = pl.ds(pl.multiple_of(me[0] * share, share), share)
    q = nt(wb[mine, :].astype(BF16), bb[...]) + g
    out[...] = q
    if diff is not None:
        diff[...] = q - arrays[0]
    row = lax.broadcasted_iota(jnp.int32, scal.shape, 0)
    num = num * (1.0 / SIDE) + total(rb[...] * q)
    den = den * (1.0 / SIDE) + total(q * q)
    scal[...] = jnp.where(row == 0, num, jnp.where(row == 1, den, 0.0))


def border_last(me, p0, p1, p2, p3, rb, wb, bb, out, scal):
    border_step(me, p0, p1, p2, p3, rb, wb, bb, out, None, scal)


def solve(target, s, out):
    out[...] = nt_full(target[...], s[...])


def step_of(parts, border):
    tile = added([part.at[:, border : border + 128] for part in parts])
    return tile[0:1] / (tile[1:2] + 1e-06)


def place(me, parts, wb, scale, old):
    share = parts[0].shape[0]
    border = wb.shape[1]
    for k, part in enumerate(parts):
        rows = pl.ds(pl.multiple_of(jnp.bitwise_xor(me, k) * share, share), share)
        if old is None:
            wb[rows, :] = part[:, :border]
        else:
            wb[rows, :] = old[rows, :] + scale * part[:, :border]


def edge_update(counts, odd, narrow, yv, ct, invt, e, w, u, first, second):
    slots, rows, _ = invt.shape
    z = slots - 1
    values = []
    for i, m in enumerate((0, z)):
        lift = nn(narrow, ct[m])
        u[i] = lift
        value = yv[i] - live_row(counts, m, rows) * nn(lift.astype(BF16), invt[m])
        w[i] = value
        values.append(value)
    put_halo(odd, values[0], nn(values[1].astype(BF16), e[z]), first, second)


def edge_first(counts, me, a0, a1, a2, a3, y, ct, invt, e, wb, w, u, first, second):
    place(me[0], (a0, a1, a2, a3), wb, None, None)
    yv = [y[0], y[1]]
    edge_update(counts, me[1], wb[...].astype(BF16), yv, ct, invt, e, w, u, first, second)


def edge_next(
    counts, me, a0, a1, a2, a3, wb_in, sol_in, rb_in, qb, y_in, p, r_in, q, ct, invt, e,
    alpha, wb, sol, rb, y, r, w, u, first, second,
):
    parts = (a0, a1, a2, a3)
    border = wb.shape[1]
    step = step_of(parts, border)
    alpha[...] = jnp.broadcast_to(step, alpha.shape)
    a = step[:, :1]
    sol[...] = sol_in[...] + a * wb_in[...]
    place(me[0], parts, wb, -a, wb_in)
    rb[...] = rb_in[...] - a * qb[...]
    yv = []
    for i in range(2):
        r[i] = r_in[i] - a * q[i]
        value = y_in[i] - a * p[i]
        y[i] = value
        yv.append(value)
    edge_update(counts, me[1], wb[...].astype(BF16), yv, ct, invt, e, w, u, first, second)


def inner_body(counts, load, narrow, w_edge, u_edge, dt, et, e, ct, c, invt, w, q, p, edge, t, g, num, den, v, u, keep):
    slots, rows, _ = invt.shape
    z = slots - 1
    v[0] = w_edge[0].astype(BF16)
    v[z] = w_edge[1].astype(BF16)

    @pl.loop(1, z)
    def _(m):
        live = live_row(counts, m, rows)
        lift = nn(narrow, ct[m])
        u[m] = lift
        value = load(m) - live * nn(lift.astype(BF16), invt[m])
        w[m - 1] = value
        v[m] = value.astype(BF16)

    if t is not None:
        t[...] = jnp.zeros_like(t)
    g[...] = jnp.zeros_like(g)
    num[...] = jnp.zeros_like(num)
    den[...] = jnp.zeros_like(den)

    @pl.loop(1, z)
    def _(m):
        live = live_row(counts, m, rows)
        value = live * (nn(v[m], dt[m]) + nn(v[m + 1], et[m]) + nn(v[m - 1], e[m - 1]) + u[m])
        num[...] += jnp.sum(keep(m) * value, 0, keepdims=True)
        den[...] += jnp.sum(value * value, 0, keepdims=True)
        if t is None:
            g[...] += nn(v[m], c[m])
        else:
            q[m - 1] = value
            back = live * nn_wide(value, invt[m])
            p[m - 1] = back
            both = nn(jnp.concatenate([back.astype(BF16), v[m]], 0), c[m])
            t[...] += both[: t.shape[0]]
            g[...] += both[t.shape[0] :]

    edge[0] = nn(v[0], dt[0]) + nn(v[1], et[0]) + u_edge[0]
    edge[1] = nn(v[z], dt[z]) + nn(v[z - 1], e[z - 1]) + u_edge[1]


def inner_first(counts, wb, w_edge, u_edge, y, r, dt, et, e, ct, c, invt, w, q, p, edge, t, g, num, den, v, u):
    inner_body(
        counts, lambda m: y[m - 1], wb[...].astype(BF16), w_edge, u_edge, dt, et, e, ct, c, invt,
        w, q, p, edge, t, g, num, den, v, u, lambda m: r[m - 1],
    )


def inner_next(
    counts, alpha, wb, w_edge, u_edge, y_in, p_in, r_in, q_in, dt, et, e, ct, c, invt,
    y, r, w, q, p, edge, t, g, num, den, v, u,
):
    a = alpha[0:1, 0:1]

    def load(m):
        y[m - 1] = y_in[m - 1] - a * p_in[m - 1]
        r[m - 1] = r_in[m - 1] - a * q_in[m - 1]
        return y[m - 1]

    inner_body(
        counts, load, wb[...].astype(BF16), w_edge, u_edge, dt, et, e, ct, c, invt,
        w, q, p, edge, t, g, num, den, v, u, lambda m: r[m - 1],
    )


def inner_last(
    counts, alpha, wb, w_edge, u_edge, y_in, p_in, r_in, q_in, dt, et, e, ct, c, invt,
    w, edge, g, num, den, v, u,
):
    a = alpha[0:1, 0:1]
    inner_body(
        counts, lambda m: y_in[m - 1] - a * p_in[m - 1], wb[...].astype(BF16), w_edge, u_edge, dt, et, e, ct, c, invt,
        w, None, None, edge, None, g, num, den, v, u, lambda m: r_in[m - 1] - a * q_in[m - 1],
    )


def outer_body(counts, me, w_edge, r_edge, edge, first, second, et, c, invt, t_in, g_in, num_in, den_in, q, p, shares, t, g):
    slots, rows, _ = invt.shape
    z = slots - 1
    ahead, behind = from_halo(me[1], first, second)
    if t is not None:
        t[...] = t_in[...]
    g[...] = g_in[...]
    num, den = total(num_in[...]), total(den_in[...])
    for i, m in enumerate((0, z)):
        live = live_row(counts, m, rows)
        other = behind if i == 0 else nn(ahead, et[z])
        value = live * (edge[i] + other)
        num += total(r_edge[i] * value)
        den += total(value * value)
        v = w_edge[i].astype(BF16)
        if t is None:
            g[...] += nn(v, c[m])
        else:
            q[i] = value
            back = live * nn_wide(value, invt[m])
            p[i] = back
            both = nn(jnp.concatenate([back.astype(BF16), v], 0), c[m])
            t[...] += both[: t.shape[0]]
            g[...] += both[t.shape[0] :]
    emit(me[0], (g,) if t is None else (t, g), shares, num, den)


def outer_step(counts, me, w_edge, r_edge, edge, first, second, et, c, invt, t_in, g_in, num, den, q, p, s0, s1, s2, s3, t, g):
    outer_body(
        counts, me, w_edge, r_edge, edge, first, second, et, c, invt, t_in, g_in, num, den, q, p, (s0, s1, s2, s3), t, g
    )


def outer_last(counts, me, w_edge, r_edge, edge, first, second, et, c, invt, g_in, num, den, s0, s1, s2, s3, g):
    outer_body(
        counts, me, w_edge, r_edge, edge, first, second, et, c, invt, None, g_in, num, den, None, None,
        (s0, s1, s2, s3), None, g,
    )


def finish(counts, a0, a1, a2, a3, wb, sol, x, al0, al1, e0, e1, e2, w0, w1, w2, out, border):
    slots, _, rows = x.shape
    step = step_of((a0, a1, a2, a3), 0)[:, :1]
    border[...] = sol[...] + step * wb[...]
    c0, c1 = al0[0:1, 0:1], al1[0:1, 0:1]
    for m in range(slots):
        if m in (0, slots - 1):
            i = 0 if m == 0 else 1
            a, b, c = e0[i], e1[i], e2[i]
        else:
            a, b, c = w0[m - 1], w1[m - 1], w2[m - 1]
        out[m] = ((x[m] * live_row(counts, m, rows) + c0 * a) + c1 * b) + step * c


def halo(first, second):
    count = lax.axis_size(AXES)
    pairs = [(i, i ^ 1) for i in range(count)]
    others = [(i, i + 1) for i in range(1, count - 1, 2)]
    first = lax.ppermute(first, AXES, pairs)
    second = lax.ppermute(second, AXES, others + [(j, i) for i, j in others])
    return first, second


def shards(
    rhs_blocks, rhs_border, start_blocks, start_border,
    diag, inverse, coupling, border_coupling, border_block, schur, counts,
):
    x = start_blocks.transpose(0, 2, 1)
    b = rhs_blocks.transpose(0, 2, 1)
    border_rhs, border_x = rhs_border.T, start_border.T
    slots, columns, rows = x.shape
    border = border_x.shape[1]
    share = columns // SIDE
    me = jnp.stack([lax.axis_index(AXES[0]), lax.rem(lax.axis_index(AXES), 2)]).astype(jnp.int32)
    state, edges = ((slots - 2, columns, rows), F32), ((2, columns, rows), F32)
    one16, wide = ((columns, rows), BF16), ((columns, border), F32)
    line, piece = ((1, rows), F32), ((share, border), F32)
    tile = ((8, 128), F32)
    keep16 = pltpu.VMEM((slots, columns, rows), BF16)
    keep32 = pltpu.VMEM((slots, columns, rows), F32)
    acc = pltpu.VMEM((columns, border), F32)

    def message(dtype, sums):
        return ((share * sums * border // 128 + tail_rows(dtype), 128), dtype)

    up, down = call(edge_start, [one16, one16], [counts, me, x, coupling[slots - 1 :]], "ssvv")
    up, down = halo(up, down)
    matrices = resident(diag, coupling, border_coupling, inverse)
    dt, et, e, ct, c, invt = matrices
    r, y, edge, t, g = call(
        inner_start,
        [state, state, edges, wide, wide],
        [counts, x, b, border_x, *matrices],
        "svvvmmmmmm",
        [keep16],
        flops=4 * 10**9,
    )
    r_edge, y_edge, *shares = call(
        outer_start,
        [edges, edges] + [message(WIRE[0], 2)] * SIDE,
        [counts, me, x, b, edge, up, down, et, c, invt, t, g],
        "ssvvvvvmmmvv",
        [acc, acc],
        flops=5 * 10**8,
    )
    parts = reduced(shares)
    rb, target = call(
        border_start, [piece, piece], [me, *parts, border_rhs, border_x, border_block], "sv" + "v" * 6
    )
    found = call(solve, [piece], [target, schur], "vv")[0]
    gathered = swapped([found] * SIDE, AXES[0])

    steps, edge_updates, updates = [], [], []
    sol = border_x
    for k in range(ITERS):
        last = k == ITERS - 1
        if k == 0:
            wb, w_edge, u_edge, up, down = call(
                edge_first,
                [wide, edges, edges, one16, one16],
                [counts, me, *gathered, y_edge, ct, invt, e],
                "ssvvvvvmmm",
                flops=5 * 10**8,
            )
        else:
            step, wb, sol, rb, y_edge, r_edge, w_edge, u_edge, up, down = call(
                edge_next,
                [tile, wide, wide, piece, edges, edges, edges, edges, one16, one16],
                [counts, me, *gathered, wb, sol, rb, qb, y_edge, p_edge, r_edge, q_edge]
                + [ct, invt, e],
                "ss" + "v" * 12 + "mmm",
                flops=5 * 10**8,
            )
            steps.append(step)
        up, down = halo(up, down)
        if k == 0:
            w, q, p, edge, t, g, num, den = call(
                inner_first,
                [state, state, state, edges, wide, wide, line, line],
                [counts, wb, w_edge, u_edge, y, r, *matrices],
                "svvvvvmmmmmm",
                [keep16, keep32],
                flops=4 * 10**9,
            )
        elif not last:
            y, r, w, q, p, edge, t, g, num, den = call(
                inner_next,
                [state, state, state, state, state, edges, wide, wide, line, line],
                [counts, step, wb, w_edge, u_edge, y, p, r, q, *matrices],
                "s" + "v" * 8 + "mmmmmm",
                [keep16, keep32],
                flops=4 * 10**9,
            )
        else:
            w, edge, g, num, den = call(
                inner_last,
                [state, edges, wide, line, line],
                [counts, step, wb, w_edge, u_edge, y, p, r, q, *matrices],
                "s" + "v" * 8 + "mmmmmm",
                [keep16, keep32],
                flops=3 * 10**9,
            )
        edge_updates.append(w_edge)
        updates.append(w)
        inputs = [counts, me, w_edge, r_edge, edge, up, down, et, c, invt]
        if not last:
            q_edge, p_edge, *shares = call(
                outer_step,
                [edges, edges] + [message(WIRE[k + 1], 2)] * SIDE,
                inputs + [t, g, num, den],
                "ssvvvvvmmmvvvv",
                [acc, acc],
                flops=5 * 10**8,
            )
            parts = reduced(shares)
            qb, diff, scal = call(
                border_step,
                [piece, piece, ((share, 128), F32)],
                [me, *parts, rb, wb, border_block],
                "s" + "v" * 7,
            )
            partner = lax.ppermute(scal, "rhs", [(0, 1), (1, 0)])
            found = call(solve, [piece], [diff, schur], "vv")[0]
            sent = jnp.concatenate([found, scal + partner], 1)
        else:
            shares = call(
                outer_last,
                [message(WIRE[k + 1], 1)] * SIDE,
                inputs + [g, num, den],
                "ssvvvvvmmmvvv",
                [acc],
                flops=3 * 10**8,
            )
            parts = reduced(shares)
            qb, scal = call(
                border_last,
                [piece, ((share, 128), F32)],
                [me, *parts, rb, wb, border_block],
                "s" + "v" * 7,
            )
            partner = lax.ppermute(scal, "rhs", [(0, 1), (1, 0)])
            sent = scal + partner
        gathered = swapped([sent] * SIDE, AXES[0])
    out, border_out = call(
        finish,
        [(x.shape, F32), wide],
        [counts, *gathered, wb, sol, x, *steps, *edge_updates, *updates],
        "s" + "v" * 15,
    )
    return out.transpose(0, 2, 1), border_out.T


def solution(mesh):
    finer = Mesh(mesh.devices.reshape(SIDE, SIDE, SIDE, mesh.shape["rhs"]), (*AXES, "rhs"))
    return jax.shard_map(
        shards,
        mesh=finer,
        in_specs=(
            P(AXES, None, "rhs"),
            P(None, "rhs"),
            P(AXES, None, "rhs"),
            P(None, "rhs"),
            P(AXES, None, None),
            P(AXES, None, None),
            P(AXES, None, None),
            P(AXES, None, None),
            P(),
            P(),
            P(AXES),
        ),
        out_specs=(P(AXES, None, "rhs"), P(None, "rhs")),
        check_vma=False,
    )
```
